128 devices in a mesh: row: 8 (over x_lo, z), col: 16 (over x_hi, y, core).
Axes of the slice: x: 4 (x_hi: 2, x_lo: 2; x = x_hi * 2 + x_lo), y: 4, z: 4, core: 2. Of those that a mesh axis runs over, the one named last changes fastest.
Arguments:
- layer_inputs: float32 [2048, 16384], P(('row', 'col')), may hold values from -60 to 60
Outputs:
- gram: float32 [16384, 16384], P('row', 'col')
The draws below stay inside these ranges and needn't reach their ends.
All inputs are finite; a program needn't handle non-finite values.
Results may differ from the reference program's by a relative error of at most 0.000073.
Values sent between devices are 32-bit elements; how exact they have to be, the bound alone decides.
No kernel may reach another device: no remote copies, remote signals or barrier semaphores. Data moves between devices by JAX's collectives and lax.ppermute only.
A program may use at most 128 MiB of HBM per device.

```python
import math
import jax
import jax.numpy as jnp
from jax import lax

D = 16384
TOKENS = 2048


def draw_layer_inputs(key, part):
    first, second, third = jax.random.split(key, 3)
    base = jnp.clip(jax.random.normal(first, (TOKENS, D), jnp.float32), -6.0, 6.0)
    feature_scale = jnp.exp(jax.random.uniform(third, (D,), jnp.float32, math.log(0.3), math.log(3.0)))
    token_scale = jnp.exp(jax.random.uniform(second, (TOKENS,), jnp.float32, math.log(0.3), math.log(3.0)))
    return (base * token_scale[:, None] * feature_scale[None, :]).astype(jnp.float32)


def setup_inputs(seed: int = 0) -> dict:
    key_of = jax.random.split(jax.random.key(seed), 2)
    layer_inputs = draw_layer_inputs(jax.random.fold_in(key_of[1], 71), 0)
    return {"layer_inputs": layer_inputs}


def reference(layer_inputs):
    product = lax.dot_general(layer_inputs, layer_inputs, (((0,), (0,)), ((), ())), precision=lax.Precision.HIGHEST, preferred_element_type=jnp.float32)
    return product / TOKENS
```

```python
import jax
import jax.numpy as jnp
from jax import lax
from jax.sharding import Mesh, PartitionSpec as P

AXES = ("xl", "z", "xh", "y", "core")


def shift(value, axis, step):
    return lax.ppermute(value, axis, [(i, (i + step) % 4) for i in range(4)])


def shift_x(value, step):
    place = [0, 2, 1, 3]
    pairs = [(place[i], place[(i + step) % 4]) for i in range(4)]
    return lax.ppermute(value, ("xl", "xh"), pairs)


def pick(value, index):
    return lax.dynamic_index_in_dim(value, index, 0, keepdims=False)


def ring(value, axis):
    half = value.shape[0] // 2
    ahead = shift(value, axis, 1)
    back = shift(value, axis, -1)
    far_a = shift(ahead[:half], axis, 1)
    far_b = shift(back[half:], axis, -1)
    return [value, ahead, back, jnp.concatenate([far_a, far_b], axis=0)]


def shards(block):
    rows, width = block.shape
    cols = width // 16
    core = lax.axis_index("core")
    y, z = lax.axis_index("y"), lax.axis_index("z")
    x = lax.axis_index("xh") * 2 + lax.axis_index("xl")

    split = block.reshape(rows, 8, 2, cols).transpose(2, 1, 0, 3)
    mine = pick(split, core)
    got = lax.ppermute(pick(split, 1 - core), "core", [(0, 1), (1, 0)])
    first = jnp.where(core == 0, mine, got)
    second = jnp.where(core == 0, got, mine)
    chip = jnp.concatenate([first, second], axis=1).reshape(2, 4, 2 * rows, cols)
    chip = chip.transpose(1, 0, 2, 3)

    def exchange(axis, here):
        parts = []
        for step in (0, 1, 3, 2):
            part = pick(chip, (here + step) % 4)
            parts.append(shift(part, axis, step) if step else part)
        return jnp.stack(parts, axis=1)

    by_y = exchange("y", y)
    by_z = exchange("z", z)

    def message(step):
        there = (x + step) % 4
        return jnp.stack([pick(by_y, there // 2), pick(by_z, there % 2)])

    own = message(0)
    left = shift_x(message(1), 1)
    right = shift_x(message(3), 3)
    far = shift_x(message(2), 2)

    tokens = 4 * 2 * rows
    total = None
    for group in ([own], [left, right], [far]):
        count = len(group)
        col_part = jnp.concatenate([g[0].reshape(tokens, cols) for g in group])
        row_part = jnp.concatenate([g[1].reshape(tokens, cols) for g in group])
        b = jnp.stack(ring(col_part, "z"))
        a = jnp.stack(ring(row_part, "y"))
        a = a.reshape(4 * count * tokens, cols)
        b = b.reshape(4, count, 4, 2 * rows, cols).transpose(2, 1, 0, 3, 4)
        b = b.reshape(4 * count * tokens, cols)
        other = lax.ppermute(a, "core", [(0, 1), (1, 0)])
        a = jnp.concatenate(
            [jnp.where(core == 0, a, other), jnp.where(core == 0, other, a)], axis=1
        )
        part = lax.dot_general(
            a,
            b,
            (((0,), (0,)), ((), ())),
            precision=lax.Precision.HIGH,
            preferred_element_type=jnp.float32,
        )
        total = part if total is None else total + part
    return total / (rows * 128)


def solution(mesh):
    fine = Mesh(mesh.devices.reshape(2, 4, 2, 4, 2), AXES)
    return jax.shard_map(
        shards,
        mesh=fine,
        in_specs=(P(AXES, None),),
        out_specs=P(("xl", "z"), ("xh", "y", "core")),
        check_vma=False,
    )
```

```python
import functools

import jax
import jax.numpy as jnp
from jax import lax
from jax.experimental import pallas as pl
from jax.experimental.pallas import tpu as pltpu
from jax.sharding import Mesh, PartitionSpec as P


AXES = ("xl", "z", "xh", "y", "core")


def move(value, step):
    pairs = []
    for z in range(4):
        for y in range(4):
            pairs.append((z * 8 + y * 2, z * 8 + (y + step) % 4 * 2))
            pairs.append((z * 8 + y * 2 + 1, (z + step) % 4 * 8 + y * 2 + 1))
    return lax.ppermute(value, ("z", "y", "core"), pairs)


def move_ring(value, step):
    pairs = []
    for z in range(4):
        for y in range(4):
            pairs.append((z * 8 + y * 2, (z + step) % 4 * 8 + y * 2))
            pairs.append((z * 8 + y * 2 + 1, z * 8 + (y + step) % 4 * 2 + 1))
    return lax.ppermute(value, ("z", "y", "core"), pairs)


def move_x(value, step):
    place = [0, 2, 1, 3]
    pairs = [(place[i], place[(i + step) % 4]) for i in range(4)]
    return lax.ppermute(value, ("xl", "xh"), pairs)


def swap(value):
    return lax.ppermute(value, "core", [(0, 1), (1, 0)])


def pick(value, index):
    return lax.dynamic_index_in_dim(value, index, 0, keepdims=False)


def after(values, deps):
    count = len(values)
    return lax.optimization_barrier(tuple(values) + tuple(deps))[:count]


def split(value):
    high = value.astype(jnp.bfloat16)
    return high, (value - high.astype(jnp.float32)).astype(jnp.bfloat16)


def gram_kernel(core_ref, *refs, scale, tile, last):
    mine, theirs = refs[:2]
    total = refs[2] if len(refs) == 5 else None
    out, right = refs[-2:]
    first = core_ref[0] == 0
    outer, inner, cols = mine.shape
    width, piece, count = cols // 2, inner // outer, outer * inner

    @pl.when(pl.program_id(0) == 0)
    def _():
        for i in range(outer):
            for j in range(outer):
                rows = pl.ds(j * piece, piece)
                ours, other = mine[i, rows, :width], theirs[i, rows, width:]
                high, low = split(jnp.where(first, ours, other))
                at = (j * outer + i) * piece
                right[pl.ds(at, piece), :] = high
                right[pl.ds(count + at, piece), :] = low
                right[pl.ds(2 * count + at, piece), :] = high

    at = pl.ds(pl.multiple_of(pl.program_id(0) * tile, tile), tile)
    left = jnp.where(first, theirs[:, :, at], mine[:, :, at]).reshape(count, tile).T
    high, low = split(left)
    part = jnp.dot(
        jnp.concatenate([high, high, low], axis=1),
        right[...],
        preferred_element_type=jnp.float32,
    )
    if total is not None:
        part = total[at, :] + part
    if last:
        out[...] = part * scale
    else:
        out[at, :] = part


def gram_add(core, mine, theirs, total, scale=None, tile=256):
    outer, inner, cols = mine.shape
    width, count = cols // 2, outer * inner
    whole = pl.BlockSpec(memory_space=pltpu.VMEM)
    args = [mine, theirs] + ([] if total is None else [total])
    last = scale is not None
    return pl.pallas_call(
        functools.partial(gram_kernel, scale=scale, tile=tile, last=last),
        out_shape=jax.ShapeDtypeStruct((cols, width), jnp.float32),
        grid_spec=pltpu.PrefetchScalarGridSpec(
            num_scalar_prefetch=1,
            grid=(cols // tile,),
            in_specs=[whole] * len(args),
            out_specs=pl.BlockSpec((tile, width), lambda m, c: (m, 0)) if last else whole,
            scratch_shapes=[pltpu.VMEM((3 * count, width), jnp.bfloat16)],
        ),
        input_output_aliases={} if last or total is None else {3: 0},
        compiler_params=pltpu.CompilerParams(vmem_limit_bytes=30 << 20),
        cost_estimate=pl.CostEstimate(
            flops=6 * count * cols * width, bytes_accessed=16 << 20, transcendentals=0
        ),
    )(core.reshape(1), *args)


def shards(block):
    rows, width = block.shape
    cols = width // 8
    core = lax.axis_index("core")
    first = core == 0
    y, z = lax.axis_index("y"), lax.axis_index("z")
    x = lax.axis_index("xh") * 2 + lax.axis_index("xl")

    got = swap(block)
    chip = jnp.concatenate([jnp.where(first, block, got), jnp.where(first, got, block)])

    def slab(index):
        starts = [(4 * h + index) * cols for h in (0, 1)]
        return [lax.dynamic_slice(chip, (0, s), (2 * rows, cols)) for s in starts]

    here = jnp.where(first, y, z)
    parts = [jnp.stack(slab(here))]
    for step in (1, 3, 2):
        parts.append(move(jnp.stack(slab((here + step) % 4)), step))
    parts = jnp.stack(parts, axis=1)

    def message(step):
        there = (x + step) % 4
        return pick(parts, jnp.where(first, there // 2, there % 2))

    tokens = 8 * rows
    own = message(0).reshape(1, tokens, cols)
    left = move_x(message(1), 1).reshape(1, tokens, cols)
    right = move_x(message(3), 3).reshape(1, tokens, cols)
    (second,) = after([message(2)], [left, right])
    far = move_x(second, 2).reshape(1, tokens, cols)

    def begin(value):
        return move_ring(value, 1), move_ring(value, -1)

    def forward(ahead, back):
        half = tokens // 2
        far_a = move_ring(ahead[:, :half], 1)
        far_b = move_ring(back[:, half:], -1)
        return far_a, far_b

    def finish(near, ends):
        near = jnp.concatenate(near)
        ends = jnp.concatenate(ends, axis=1)
        theirs = jnp.concatenate([swap(near), swap(ends)])
        return jnp.concatenate([near, ends]), theirs

    def gather(value, ahead, back, far_a, far_b, index):
        ends = jnp.concatenate([far_a[index], far_b[index]])
        return jnp.stack([value[index], ahead[index], back[index], ends])

    own_1 = begin(own)
    own_2 = forward(*own_1)
    left_1 = begin(left)
    right_1 = begin(right)
    mine = gather(own, *own_1, *own_2, 0)
    total = gram_add(core, mine, swap(mine), None)
    left_1 = after(left_1, [total])
    right_1 = after(right_1, [total])
    (far,) = after([far], [total])
    left_2 = forward(*left_1)
    right_2 = forward(*right_1)
    far_1 = begin(far)
    mine = gather(left, *left_1, *left_2, 0)
    theirs = swap(mine)
    right, *sides = after([right, *right_1, *right_2], [mine])
    mine_r = gather(right, *sides, 0)
    theirs_r = swap(mine_r)
    total = gram_add(core, mine, theirs, total)
    far, *far_1 = after([far, *far_1], [total])
    far_2 = forward(*far_1)
    total = gram_add(core, mine_r, theirs_r, total, tile=512)
    far_2 = after(far_2, [total])
    return gram_add(core, *finish([far, *far_1], far_2), total, 1 / (rows * 128))


def solution(mesh):
    fine = Mesh(mesh.devices.reshape(2, 4, 2, 4, 2), AXES)

    return jax.shard_map(
        shards,
        mesh=fine,
        in_specs=(P(AXES, None),),
        out_specs=P(("xl", "z"), ("xh", "y", "core")),
        check_vma=False,
    )
```

```python
import functools

import jax
import jax.numpy as jnp
from jax import lax
from jax.experimental import pallas as pl
from jax.experimental.pallas import tpu as pltpu
from jax.sharding import Mesh, PartitionSpec as P


AXES = ("xl", "z", "xh", "y", "core")


def move(value, step):
    pairs = []
    for z in range(4):
        for y in range(4):
            pairs.append((z * 8 + y * 2, z * 8 + (y + step) % 4 * 2))
            pairs.append((z * 8 + y * 2 + 1, (z + step) % 4 * 8 + y * 2 + 1))
    return lax.ppermute(value, ("z", "y", "core"), pairs)


def move_ring(value, step):
    pairs = []
    for z in range(4):
        for y in range(4):
            pairs.append((z * 8 + y * 2, (z + step) % 4 * 8 + y * 2))
            pairs.append((z * 8 + y * 2 + 1, z * 8 + (y + step) % 4 * 2 + 1))
    return lax.ppermute(value, ("z", "y", "core"), pairs)


def move_x(value, step):
    place = [0, 2, 1, 3]
    pairs = [(place[i], place[(i + step) % 4]) for i in range(4)]
    return lax.ppermute(value, ("xl", "xh"), pairs)


def swap(value):
    return lax.ppermute(value, "core", [(0, 1), (1, 0)])


def pick(value, index):
    return lax.dynamic_index_in_dim(value, index, 0, keepdims=False)


def after(values, deps):
    count = len(values)
    return lax.optimization_barrier(tuple(values) + tuple(deps))[:count]


def split(value):
    high = value.astype(jnp.bfloat16)
    return high, (value - high.astype(jnp.float32)).astype(jnp.bfloat16)


def gram_kernel(core_ref, *refs, scale, tile, last):
    mine, theirs = refs[:2], refs[2:4]
    total = refs[4] if len(refs) == 7 else None
    out, right = refs[-2:]
    first = core_ref[0] == 0
    inner, cols = mine[0].shape[1:]
    lengths = [part.shape[0] for part in mine]
    outer = sum(lengths)
    width, piece, count = cols // 2, inner // outer, outer * inner
    where = [(k, i) for k, length in enumerate(lengths) for i in range(length)]

    @pl.when(pl.program_id(0) == 0)
    def _():
        for i, (k, n) in enumerate(where):
            for j in range(outer):
                rows = pl.ds(j * piece, piece)
                ours, other = mine[k][n, rows, :width], theirs[k][n, rows, width:]
                high, low = split(jnp.where(first, ours, other))
                at = (j * outer + i) * piece
                right[pl.ds(at, piece), :] = high
                right[pl.ds(count + at, piece), :] = low
                right[pl.ds(2 * count + at, piece), :] = high

    at = pl.ds(pl.multiple_of(pl.program_id(0) * tile, tile), tile)
    left = jnp.concatenate(
        [
            jnp.where(first, theirs[k][:, :, at], mine[k][:, :, at]).reshape(-1, tile)
            for k in range(len(mine))
        ]
    ).T
    high, low = split(left)
    part = jnp.dot(
        jnp.concatenate([high, high, low], axis=1),
        right[...],
        preferred_element_type=jnp.float32,
    )
    if total is not None:
        part = total[at, :] + part
    if last:
        out[...] = part * scale
    else:
        out[at, :] = part


def gram_add(core, mine, theirs, total, scale=None, tile=256):
    outer, (inner, cols) = sum(m.shape[0] for m in mine), mine[0].shape[1:]
    width, count = cols // 2, outer * inner
    whole = pl.BlockSpec(memory_space=pltpu.VMEM)
    args = [*mine, *theirs] + ([] if total is None else [total])
    last = scale is not None
    return pl.pallas_call(
        functools.partial(gram_kernel, scale=scale, tile=tile, last=last),
        out_shape=jax.ShapeDtypeStruct((cols, width), jnp.float32),
        grid_spec=pltpu.PrefetchScalarGridSpec(
            num_scalar_prefetch=1,
            grid=(cols // tile,),
            in_specs=[whole] * len(args),
            out_specs=pl.BlockSpec((tile, width), lambda m, c: (m, 0)) if last else whole,
            scratch_shapes=[pltpu.VMEM((3 * count, width), jnp.bfloat16)],
        ),
        input_output_aliases={} if last or total is None else {5: 0},
        compiler_params=pltpu.CompilerParams(vmem_limit_bytes=12 << 20),
        cost_estimate=pl.CostEstimate(
            flops=6 * count * cols * width, bytes_accessed=16 << 20, transcendentals=0
        ),
    )(core.reshape(1), *args)


def shards(block):
    rows, width = block.shape
    cols = width // 8
    core = lax.axis_index("core")
    first = core == 0
    y, z = lax.axis_index("y"), lax.axis_index("z")
    x = lax.axis_index("xh") * 2 + lax.axis_index("xl")

    got = swap(block)
    chip = jnp.concatenate([jnp.where(first, block, got), jnp.where(first, got, block)])

    def slab(index):
        starts = [(4 * h + index) * cols for h in (0, 1)]
        return [lax.dynamic_slice(chip, (0, s), (2 * rows, cols)) for s in starts]

    here = jnp.where(first, y, z)
    parts = [jnp.stack(slab(here))]
    for step in (1, 3, 2):
        parts.append(move(jnp.stack(slab((here + step) % 4)), step))
    parts = jnp.stack(parts, axis=1)

    def message(step):
        there = (x + step) % 4
        return pick(parts, jnp.where(first, there // 2, there % 2))

    tokens = 8 * rows
    own = message(0).reshape(1, tokens, cols)
    plus, minus = message(1), message(3)

    def sides(part):
        got = [move_x(plus[:, part], 1), move_x(minus[:, part], 3)]
        return jnp.concatenate(got, axis=1).reshape(1, tokens, cols)

    left = sides(slice(0, rows))
    right = sides(slice(rows, 2 * rows))
    (second,) = after([message(2)], [right])
    far = move_x(second, 2).reshape(1, tokens, cols)

    def begin(value):
        return move_ring(value, 1), move_ring(value, -1)

    def forward(ahead, back):
        half = tokens // 2
        far_a = move_ring(ahead[:, :half], 1)
        far_b = move_ring(back[:, half:], -1)
        return far_a, far_b

    def finish(near, ends):
        mine = (jnp.concatenate(near), jnp.concatenate(ends, axis=1))
        return mine, (swap(mine[0]), swap(mine[1]))

    own_1 = begin(own)
    own_2 = forward(*own_1)
    left_1 = begin(left)
    right_1 = begin(right)
    total = gram_add(core, *finish([own, *own_1], own_2), None)
    left_1 = after(left_1, [total])
    left_2 = forward(*left_1)
    right_1 = after(right_1, left_1)
    right_2 = forward(*right_1)
    (far,) = after([far], right_1)
    far_1 = begin(far)
    total = gram_add(core, *finish([left, *left_1], left_2), total)
    right_2 = after(right_2, [total])
    far_1 = after(far_1, [total])
    far_2 = forward(*far_1)
    total = gram_add(core, *finish([right, *right_1], right_2), total)
    far_2 = after(far_2, [total])
    return gram_add(core, *finish([far, *far_1], far_2), total, 1 / (rows * 128))


def solution(mesh):
    fine = Mesh(mesh.devices.reshape(2, 4, 2, 4, 2), AXES)

    return jax.shard_map(
        shards,
        mesh=fine,
        in_specs=(P(AXES, None),),
        out_specs=P(("xl", "z"), ("xh", "y", "core")),
        check_vma=False,
    )
```

```python
import functools

import jax
import jax.numpy as jnp
from jax import lax
from jax.experimental import pallas as pl
from jax.experimental.pallas import tpu as pltpu
from jax.sharding import Mesh, PartitionSpec as P


AXES = ("xl", "z", "xh", "y", "core")


def move(value, step):
    pairs = []
    for z in range(4):
        for y in range(4):
            pairs.append((z * 8 + y * 2, z * 8 + (y + step) % 4 * 2))
            pairs.append((z * 8 + y * 2 + 1, (z + step) % 4 * 8 + y * 2 + 1))
    return lax.ppermute(value, ("z", "y", "core"), pairs)


def move_ring(value, step):
    pairs = []
    for z in range(4):
        for y in range(4):
            pairs.append((z * 8 + y * 2, (z + step) % 4 * 8 + y * 2))
            pairs.append((z * 8 + y * 2 + 1, z * 8 + (y + step) % 4 * 2 + 1))
    return lax.ppermute(value, ("z", "y", "core"), pairs)


def move_x(value, step):
    place = [0, 2, 1, 3]
    pairs = [(place[i], place[(i + step) % 4]) for i in range(4)]
    return lax.ppermute(value, ("xl", "xh"), pairs)


def swap(value):
    return lax.ppermute(value, "core", [(0, 1), (1, 0)])


def pick(value, index):
    return lax.dynamic_index_in_dim(value, index, 0, keepdims=False)


def after(values, deps):
    count = len(values)
    return lax.optimization_barrier(tuple(values) + tuple(deps))[:count]


def split(value):
    high = value.astype(jnp.bfloat16)
    return high, (value - high.astype(jnp.float32)).astype(jnp.bfloat16)


def gram_kernel(core_ref, *refs, scale, tile, last):
    mine, theirs = refs[:2], refs[2:4]
    total = refs[4] if len(refs) == 7 else None
    out, right = refs[-2:]
    first = core_ref[0] == 0
    inner, cols = mine[0].shape[1:]
    lengths = [part.shape[0] for part in mine]
    outer = sum(lengths)
    width, piece, count = cols // 2, inner // outer, outer * inner
    where = [(k, i) for k, length in enumerate(lengths) for i in range(length)]

    @pl.when(pl.program_id(0) == 0)
    def _():
        for i, (k, n) in enumerate(where):
            for j in range(outer):
                rows = pl.ds(j * piece, piece)
                ours, other = mine[k][n, rows, :width], theirs[k][n, rows, width:]
                high, low = split(jnp.where(first, ours, other))
                at = (j * outer + i) * piece
                right[pl.ds(at, piece), :] = high
                right[pl.ds(count + at, piece), :] = low
                right[pl.ds(2 * count + at, piece), :] = high

    at = pl.ds(pl.multiple_of(pl.program_id(0) * tile, tile), tile)
    left = jnp.concatenate(
        [
            jnp.where(first, theirs[k][:, :, at], mine[k][:, :, at]).reshape(-1, tile)
            for k in range(len(mine))
        ]
    ).T
    high, low = split(left)
    part = jnp.dot(
        jnp.concatenate([high, high, low], axis=1),
        right[...],
        preferred_element_type=jnp.float32,
    )
    if total is not None:
        part = total[at, :] + part
    if last:
        out[...] = part * scale
    else:
        out[at, :] = part


def gram_add(core, mine, theirs, total, scale=None, tile=256):
    outer, (inner, cols) = sum(m.shape[0] for m in mine), mine[0].shape[1:]
    width, count = cols // 2, outer * inner
    whole = pl.BlockSpec(memory_space=pltpu.VMEM)
    args = [*mine, *theirs] + ([] if total is None else [total])
    last = scale is not None
    return pl.pallas_call(
        functools.partial(gram_kernel, scale=scale, tile=tile, last=last),
        out_shape=jax.ShapeDtypeStruct((cols, width), jnp.float32),
        grid_spec=pltpu.PrefetchScalarGridSpec(
            num_scalar_prefetch=1,
            grid=(cols // tile,),
            in_specs=[whole] * len(args),
            out_specs=pl.BlockSpec((tile, width), lambda m, c: (m, 0)) if last else whole,
            scratch_shapes=[pltpu.VMEM((3 * count, width), jnp.bfloat16)],
        ),
        input_output_aliases={} if last or total is None else {5: 0},
        compiler_params=pltpu.CompilerParams(vmem_limit_bytes=12 << 20),
        cost_estimate=pl.CostEstimate(
            flops=6 * count * cols * width, bytes_accessed=16 << 20, transcendentals=0
        ),
    )(core.reshape(1), *args)


def shards(block):
    rows, width = block.shape
    cols = width // 8
    core = lax.axis_index("core")
    first = core == 0
    y, z = lax.axis_index("y"), lax.axis_index("z")
    x = lax.axis_index("xh") * 2 + lax.axis_index("xl")

    got = swap(block)
    chip = jnp.concatenate([jnp.where(first, block, got), jnp.where(first, got, block)])

    def slab(index):
        starts = [(4 * h + index) * cols for h in (0, 1)]
        return [lax.dynamic_slice(chip, (0, s), (2 * rows, cols)) for s in starts]

    here = jnp.where(first, y, z)
    parts = [jnp.stack(slab(here))]
    for step in (1, 3, 2):
        parts.append(move(jnp.stack(slab((here + step) % 4)), step))
    parts = jnp.stack(parts, axis=1)

    def message(step):
        there = (x + step) % 4
        return pick(parts, jnp.where(first, there // 2, there % 2))

    tokens = 8 * rows
    own = message(0).reshape(1, tokens, cols)
    plus, minus = message(1), message(3)

    def sides(part):
        got = [move_x(plus[:, part], 1), move_x(minus[:, part], 3)]
        return jnp.concatenate(got, axis=1).reshape(1, tokens, cols)

    left = sides(slice(0, rows))
    right = sides(slice(rows, 2 * rows))
    (second,) = after([message(2)], [right])
    far = move_x(second, 2).reshape(1, tokens, cols)

    def begin(value):
        return move_ring(value, 1), move_ring(value, -1)

    def forward(ahead, back):
        half = tokens // 2
        far_a = move_ring(ahead[:, :half], 1)
        far_b = move_ring(back[:, half:], -1)
        return far_a, far_b

    def finish(near, ends):
        mine = (jnp.concatenate(near), jnp.concatenate(ends, axis=1))
        return mine, (swap(mine[0]), swap(mine[1]))

    def add(slices, total, scale=None):
        return gram_add(core, *slices, total, scale)

    own_1 = begin(own)
    own_2 = forward(*own_1)
    left_1 = begin(left)
    right_1 = begin(right)
    left_2 = forward(*left_1)
    total = add(finish([own, *own_1], own_2), None)
    right_1 = after(right_1, [total])
    right_2 = forward(*right_1)
    (far,) = after([far], [total])
    far_1 = begin(far)
    total = add(finish([left, *left_1], left_2), total)
    right_2 = after(right_2, left_2)
    far_1 = after(far_1, [total])
    far_2 = forward(*far_1)
    total = add(finish([right, *right_1], right_2), total)
    far_2 = after(far_2, [total])
    return add(finish([far, *far_1], far_2), total, 1 / (rows * 128))


def solution(mesh):
    fine = Mesh(mesh.devices.reshape(2, 4, 2, 4, 2), AXES)

    return jax.shard_map(
        shards,
        mesh=fine,
        in_specs=(P(AXES, None),),
        out_specs=P(("xl", "z"), ("xh", "y", "core")),
        check_vma=False,
    )
```
